512 devices in a mesh: prow: 16 (over y, x), pcol: 32 (over z, core).
Axes of the slice: x: 4, y: 4, z: 16, core: 2. Of those that a mesh axis runs over, the one named last changes fastest.
Arguments:
- factor_tiles: bfloat16 [16, 1024, 1, 16, 1024], P(None, 'pcol', None, 'prow'), may hold values from -0.03125 to 0.03125
- inverse_blocks: bfloat16 [1, 16, 1024, 1024], P(None, 'prow'), may hold values from -1 to 3, as said below
- demand: bfloat16 [16, 1024, 256], P(None, 'pcol'), may hold values from -6 to 6
Outputs:
- solved: bfloat16 [1, 16, 1024, 256], P(None, 'prow')
The draws below stay inside these ranges and needn't reach their ends.
Inputs may be any that keep to these rules, and one draw needn't show every extreme that they name: `inverse_blocks`: each [1024, 1024] block is lower triangular with a positive diagonal.
All inputs are finite; a program needn't handle non-finite values.
Results may differ from the reference program's by a relative error of at most 0.0075.
Values may be sent and summed in bfloat16 or wider, within the bound.
A program may use at most 64 MiB of HBM per device.

```python
import jax
import jax.numpy as jnp
from jax import lax

NB = 1024
CL = 1
NRHS = 256
NBLK = 16
ORDER = 16384
N_PROW = 16


def draw_inverse_blocks(key, part):
    key_diag, key_lower = jax.random.split(key)
    shape = (CL, NBLK // CL, NB, NB)
    diagonal = jnp.exp(jax.random.uniform(key_diag, shape[:3], jnp.float32, math_log(0.5), math_log(2.0)))
    lower = jax.random.truncated_normal(key_lower, -4.0, 4.0, shape, jnp.float32) * (0.6 / NB ** 0.5)
    row_ids = lax.broadcasted_iota(jnp.int32, (NB, NB), 0)
    column_ids = lax.broadcasted_iota(jnp.int32, (NB, NB), 1)
    strict = (row_ids > column_ids).astype(jnp.float32)
    identity = (row_ids == column_ids).astype(jnp.float32)
    return (lower * strict + diagonal[..., :, None] * identity).astype(jnp.bfloat16)


def math_log(value):
    return jnp.log(jnp.float32(value))


def steps_of(own_key, shape, pieces, low, top_value):
    def one(position, shards_of):
        draws = jax.random.uniform(jax.random.fold_in(jax.random.fold_in(own_key, 6), position), (shards_of,), jnp.float32, low / len(pieces), top_value / len(pieces))
        return jnp.repeat(jnp.exp(draws), shape[position] // shards_of).reshape((-1,) + (1,) * (len(shape) - position - 1))

    factor_of = one(*pieces[0])
    for cut in pieces[1:]:
        factor_of = factor_of * one(*cut)
    return factor_of


def centred(rng, dims, spread, limit, shards=(), held_as=jnp.bfloat16):
    values = spread * jax.random.normal(rng, dims, jnp.float32)
    if shards:
        values = values * steps_of(rng, dims, shards, -0.22, 0.18)
    return jnp.clip(values, -limit, limit).astype(held_as)


def setup_inputs(seed: int = 0) -> dict:
    arg_keys = jax.random.split(jax.random.key(seed), 4)
    factor_tiles = centred(arg_keys[0], (NBLK, NB, CL, N_PROW, NB), (2 * ORDER) ** -0.5, 0.03125, ((1, 32), (3, 16)))
    inverse_blocks = draw_inverse_blocks(jax.random.fold_in(arg_keys[3], 71), 0)
    demand = centred(arg_keys[2], (NBLK, NB, NRHS), 1.0, 6.0, ((1, 32),))
    return {"factor_tiles": factor_tiles, "inverse_blocks": inverse_blocks, "demand": demand}


def reference(factor_tiles, inverse_blocks, demand):
    row_tiles = factor_tiles.reshape(NBLK, NB, NBLK * NB)
    inverse = inverse_blocks.reshape(NBLK, NB, NB)

    def advance(step_index, solved):
        current = lax.dynamic_index_in_dim(row_tiles, step_index, 0, keepdims=False)
        partial_sum = jnp.dot(current, solved.reshape(NBLK * NB, NRHS), preferred_element_type=jnp.float32)
        target = lax.dynamic_index_in_dim(demand, step_index, 0, keepdims=False)
        residual = (target.astype(jnp.float32) - partial_sum).astype(jnp.bfloat16)
        block_inv = lax.dynamic_index_in_dim(inverse, step_index, 0, keepdims=False)
        result = jnp.dot(block_inv, residual, preferred_element_type=jnp.float32).astype(jnp.bfloat16)
        return lax.dynamic_update_index_in_dim(solved, result, step_index, 0)

    solved = lax.fori_loop(0, NBLK, advance, jnp.zeros((NBLK, NB, NRHS), jnp.bfloat16))
    return solved.reshape(CL, N_PROW, NB, NRHS)
```

```python
import functools

import jax
import jax.numpy as jnp
from jax import lax
from jax.experimental import pallas as pl
from jax.experimental.pallas import tpu as pltpu
from jax.sharding import PartitionSpec as P

MESH = pl.DeviceIdType.MESH
NT = (((1,), (1,)), ((), ()))


def dot_nt(lhs, rhs):
    return lax.dot_general(lhs, rhs, NT, preferred_element_type=jnp.float32)


def kernel(
    n, nz, cols, rows,
    tiles, inverse, demand, out,
    gathered, diag, diag_split, asked, base, partial, sol, sol_split, sol_far, contrib, result,
    own_sem, own_send, right_send, right_recv, left_send, left_recv,
    ask_own, ask_rsend, ask_rrecv, ask_lsend, ask_lrecv,
    diag_sem, base_send, base_recv, part_send, part_recv,
    far_send, far_recv, out_send, out_recv, swap_send, swap_recv,
):
    n2, hops = n // 2, nz // 2
    w = lax.axis_index("prow")
    q = lax.axis_index("pcol")
    z, c = q // 2, q % 2
    other = q + 1 - 2 * c
    right = lax.rem(z + 1, nz) * 2 + c
    left = lax.rem(z + nz - 1, nz) * 2 + c
    low = w < n2
    j = jnp.where(low, w, n - 1 - w)
    far = n - 1 - w
    count = jnp.where(low, n2, n2 - 1)
    shared = jnp.where(low, n2 - j, n2 - 1 - j)
    first = jnp.where(low, j + 1, j + 2)
    half = gathered.shape[1] * rows

    def remote(src, dst, send, recv, device):
        return pltpu.make_async_remote_copy(
            src_ref=src, dst_ref=dst, send_sem=send, recv_sem=recv,
            device_id=device, device_id_type=MESH,
        )

    def row_of(k):
        return jnp.where(k < shared, first + 2 * k, jnp.where(low, n2, n2 + 1) + k)

    def is_moved(k):
        return jnp.logical_and(jnp.logical_not(low), k < shared)

    def local_tile(k):
        return pltpu.make_async_copy(tiles.at[row_of(k)], gathered.at[k, z], own_sem.at[k])

    def moved_tile(k, row):
        return remote(tiles.at[row], gathered.at[k, z], own_send.at[k], own_sem.at[k], (far, q))

    def ring_right(k, h):
        o = lax.rem(z - h + nz, nz)
        return remote(gathered.at[k, o], gathered.at[k, o], right_send.at[k, h], right_recv.at[k, h], (w, right))

    def ring_left(k, h):
        o = lax.rem(z + h, nz)
        return remote(gathered.at[k, o], gathered.at[k, o], left_send.at[k, h], left_recv.at[k, h], (w, left))

    def ring_right_in(k, h):
        o = lax.rem(z - h - 1 + nz, nz)
        return remote(gathered.at[k, o], gathered.at[k, o], right_send.at[k, h], right_recv.at[k, h], (w, right))

    def ring_left_in(k, h):
        o = lax.rem(z + h + 1, nz)
        return remote(gathered.at[k, o], gathered.at[k, o], left_send.at[k, h], left_recv.at[k, h], (w, left))

    def ask_right(h):
        o = lax.rem(z - h + nz, nz)
        return remote(asked.at[o], asked.at[o], ask_rsend.at[h], ask_rrecv.at[h], (w, right))

    def ask_left(h):
        o = lax.rem(z + h, nz)
        return remote(asked.at[o], asked.at[o], ask_lsend.at[h], ask_lrecv.at[h], (w, left))

    def ask_right_in(h):
        o = lax.rem(z - h - 1 + nz, nz)
        return remote(asked.at[o], asked.at[o], ask_rsend.at[h], ask_rrecv.at[h], (w, right))

    def ask_left_in(h):
        o = lax.rem(z + h + 1, nz)
        return remote(asked.at[o], asked.at[o], ask_lsend.at[h], ask_lrecv.at[h], (w, left))

    base_copy = remote(base.at[c], base.at[c], base_send, base_recv, (w, other))
    base_in = remote(base.at[1 - c], base.at[1 - c], base_send, base_recv, (w, other))
    far_copy = remote(sol, sol_far, far_send, far_recv, (far, q))
    diag_copy = pltpu.make_async_copy(inverse, diag, diag_sem)
    ask_copy = pltpu.make_async_copy(demand.at[w], asked.at[z], ask_own)

    def part_copy(k, i, col, core):
        return remote(contrib.at[k], partial.at[col, c], part_send.at[k, core], part_recv.at[col, c], (i, 2 * z + core))

    def part_in(col, core):
        return remote(contrib.at[0], partial.at[col, core], part_send.at[0, 0], part_recv.at[col, core], (w, other))

    ask_copy.start()
    for k in range(n2):
        @pl.when(jnp.logical_and(k < count, jnp.logical_not(is_moved(k))))
        def _():
            local_tile(k).start()
    diag_copy.start()

    barrier = pltpu.get_barrier_semaphore()
    me = 2 * w + c

    def greet_plane(d, carry):
        t = lax.rem(me + d, 2 * n)
        pl.semaphore_signal(barrier, inc=1, device_id=(t // 2, 2 * z + t % 2), device_id_type=MESH)
        return carry

    def greet_ring(d, carry):
        t = lax.rem(z + d, nz)
        pl.semaphore_signal(barrier, inc=1, device_id=(w, 2 * t + c), device_id_type=MESH)
        return carry

    lax.fori_loop(1, 2 * n, greet_plane, 0)
    lax.fori_loop(1, nz, greet_ring, 0)
    pl.semaphore_wait(barrier, 2 * n - 1 + nz - 1)

    def gives(k):
        return jnp.logical_and(low, k < n2 - 1 - j)

    for k in range(n2 - 1):
        @pl.when(gives(k))
        def _():
            moved_tile(k, w + 2 + 2 * k).start()
    ask_copy.wait()

    def solve(i):
        @pl.when(i == 0)
        def _():
            diag_split_now()

        base_in.wait_recv()

        def add(col, acc):
            a, b = acc
            part_in(col, 0).wait_recv()
            part_in(col, 1).wait_recv()
            return a + partial[col, 0].astype(jnp.float32), b + partial[col, 1].astype(jnp.float32)

        zero = jnp.zeros((cols, half), jnp.float32)
        a, b = lax.fori_loop(0, i, add, (zero, zero))
        a = (base[0].astype(jnp.float32) - a).astype(jnp.bfloat16)
        b = (base[1].astype(jnp.float32) - b).astype(jnp.bfloat16)
        y = (dot_nt(a, diag_split[0]) + dot_nt(b, diag_split[1])).astype(jnp.bfloat16)
        sol[...] = y
        sol_split[0] = y[:, :half]
        sol_split[1] = y[:, half:]

        @pl.when(w < n2 - 1)
        def _():
            far_copy.start()

    def diag_split_now():
        diag_copy.wait()
        span, lane = 4 * rows * 2, 4 * rows
        m = lax.broadcasted_iota(jnp.int32, (span, span), 0)
        t = lax.broadcasted_iota(jnp.int32, (span, span), 1)
        core, t = t // lane, t % lane
        pick = (m == (t // rows) * (2 * rows) + core * rows + t % rows).astype(jnp.bfloat16)
        for u in range(diag.shape[1] // span):
            moved = jnp.dot(
                diag[:, u * span:(u + 1) * span], pick, preferred_element_type=jnp.float32
            ).astype(jnp.bfloat16)
            diag_split[0, :, u * lane:(u + 1) * lane] = moved[:, :lane]
            diag_split[1, :, u * lane:(u + 1) * lane] = moved[:, lane:]

    def apply(i, k, use_far):
        col = jnp.where(use_far, far, w)

        @pl.when(jnp.logical_and(use_far, k == 0))
        def _():
            far_copy.wait_recv()

        y = jnp.where(use_far, sol_far[...], sol[...])
        tile = gathered[k].reshape(half, gathered.shape[3])
        contrib[k] = dot_nt(y, tile).astype(jnp.bfloat16)
        part_copy(k, i, col, 0).start()
        part_copy(k, i, col, 1).start()

    def row_step(i):
        shared_end = first + 2 * (shared - 1)
        off = i - first
        near = jnp.logical_and(
            jnp.logical_and(off >= 0, i <= shared_end), lax.rem(off + 2 * n, 2) == 0
        )
        late = i > jnp.where(low, n - 1 - j, w)
        k = jnp.where(near, off // 2, i - jnp.where(low, n2, n2 + 1))
        k = jnp.where(jnp.logical_or(near, late), k, 0)

        @pl.when(jnp.logical_or(near, late))
        def _():
            apply(i, k, is_moved(k))

        @pl.when(i == w)
        def _():
            solve(i)

    def ring_slot(t):
        for m in range(hops // 2, -1, -1):
            k = t // 2 - m
            h = t % 2 + 2 * m
            live = jnp.logical_and(jnp.logical_and(k >= 0, k < count), h <= hops)

            @pl.when(jnp.logical_and(live, h == 0))
            def _():
                @pl.when(is_moved(k))
                def _():
                    moved_tile(k, 0).wait_recv()

                @pl.when(jnp.logical_not(is_moved(k)))
                def _():
                    local_tile(k).wait()

                ring_right(k, 0).start()
                ring_left(k, 0).start()

            @pl.when(jnp.logical_and(live, jnp.logical_and(h > 0, h < hops)))
            def _():
                ring_right_in(k, h - 1).wait_recv()
                ring_right(k, h).start()
                ring_left_in(k, h - 1).wait_recv()

                @pl.when(h < hops - 1)
                def _():
                    ring_left(k, h).start()

            @pl.when(jnp.logical_and(live, h == hops))
            def _():
                ring_right_in(k, h - 1).wait_recv()

    def ask_slot(t):
        @pl.when(t == 0)
        def _():
            ask_right(0).start()
            ask_left(0).start()

        @pl.when(jnp.logical_and(t > 0, t < hops))
        def _():
            ask_right_in(t - 1).wait_recv()
            ask_right(t).start()
            ask_left_in(t - 1).wait_recv()

            @pl.when(t < hops - 1)
            def _():
                ask_left(t).start()

        @pl.when(t == hops - 1)
        def _():
            ask_right_in(t).wait_recv()
            wide = asked.shape[2]
            pick = (
                lax.broadcasted_iota(jnp.int32, (cols, wide), 1)
                == cols * z + lax.broadcasted_iota(jnp.int32, (cols, wide), 0)
            ).astype(jnp.bfloat16)
            base[c] = dot_nt(pick, asked[...].reshape(half, wide)).astype(jnp.bfloat16)
            base_copy.start()

        @pl.when(jnp.logical_and(t == 2, w > 0))
        def _():
            diag_split_now()

    def slot(t, carry):
        ask_slot(t)
        ring_slot(t)
        i = t - (hops - 1)

        @pl.when(i >= 0)
        def _():
            row_step(i)

        return carry

    lax.fori_loop(0, n - 1 + hops, slot, 0)

    def out_copy(d):
        t = lax.rem(z + d, nz)
        return remote(sol_split.at[c], result.at[c, z], out_send.at[d], out_recv.at[d], (w, 2 * t + c))

    def out_in(d):
        t = lax.rem(z - d + nz, nz)
        return remote(sol_split.at[c], result.at[c, t], out_send.at[d], out_recv.at[d], (w, 2 * t + c))

    for d in range(1, hops + 1):
        out_copy(hops + 1 - d).start()
        if hops + d < nz:
            out_copy(hops + d).start()
    result[c, z] = sol_split[c]
    for d in range(1, nz):
        out_in(d).wait_recv()
    swap = remote(result.at[c], result.at[c], swap_send, swap_recv, (w, other))
    swap.start()

    for k in range(n2 - 1):
        @pl.when(gives(k))
        def _():
            moved_tile(k, w + 2 + 2 * k).wait_send()
    for k in range(n2):
        @pl.when(k < count)
        def _():
            for h in range(hops):
                ring_right(k, h).wait_send()
            for h in range(hops - 1):
                ring_left(k, h).wait_send()
            part_copy(k, 0, 0, 0).wait_send()
            part_copy(k, 0, 0, 1).wait_send()
    for h in range(hops):
        ask_right(h).wait_send()
    for h in range(hops - 1):
        ask_left(h).wait_send()
    base_copy.wait_send()

    @pl.when(w < n2 - 1)
    def _():
        far_copy.wait_send()

    for d in range(1, nz):
        out_copy(d).wait_send()
    swap.wait_send()
    remote(result.at[1 - c], result.at[1 - c], swap_send, swap_recv, (w, other)).wait_recv()
    for s in range(2):
        out[:, s * half:(s + 1) * half] = result[s].reshape(nz * cols, half)


def on_device(factor_tiles, inverse_blocks, demand):
    n, rows, _, _, width = factor_tiles.shape
    nz = lax.axis_size("pcol") // 2
    wide = demand.shape[2]
    cols = wide // nz
    half = width // 2
    n2, hops = n // 2, nz // 2
    dma = pltpu.SemaphoreType.DMA
    out = pl.pallas_call(
        functools.partial(kernel, n, nz, cols, rows),
        out_shape=jax.ShapeDtypeStruct((wide, width), jnp.bfloat16),
        in_specs=[pl.BlockSpec(memory_space=pl.ANY)] * 3,
        out_specs=pl.BlockSpec(memory_space=pltpu.VMEM),
        scratch_shapes=[
            pltpu.VMEM((n2, nz, rows, width), jnp.bfloat16),
            pltpu.VMEM((width, width), jnp.bfloat16),
            pltpu.VMEM((2, width, half), jnp.bfloat16),
            pltpu.VMEM((nz, rows, wide), jnp.bfloat16),
            pltpu.VMEM((2, cols, half), jnp.bfloat16),
            pltpu.VMEM((n, 2, cols, half), jnp.bfloat16),
            pltpu.VMEM((cols, width), jnp.bfloat16),
            pltpu.VMEM((2, cols, half), jnp.bfloat16),
            pltpu.VMEM((cols, width), jnp.bfloat16),
            pltpu.VMEM((n2, cols, half), jnp.bfloat16),
            pltpu.VMEM((2, nz, cols, half), jnp.bfloat16),
            dma((n2,)), dma((n2,)),
            dma((n2, hops)), dma((n2, hops)), dma((n2, hops - 1)), dma((n2, hops - 1)),
            dma, dma((hops,)), dma((hops,)), dma((hops - 1,)), dma((hops - 1,)),
            dma, dma, dma, dma((n2, 2)), dma((n, 2)),
            dma, dma, dma((nz,)), dma((nz,)), dma, dma,
        ],
        compiler_params=pltpu.CompilerParams(
            collective_id=0, has_side_effects=True, vmem_limit_bytes=48 * 1024 * 1024
        ),
    )(
        factor_tiles.reshape(n, rows, width),
        inverse_blocks.reshape(width, width),
        demand,
    )
    return out.T.reshape(1, 1, width, wide)


def solution(mesh):
    placed = (
        P(None, "pcol", None, "prow", None),
        P(None, "prow", None, None),
        P(None, "pcol", None),
    )
    return jax.shard_map(
        on_device,
        mesh=mesh,
        in_specs=placed,
        out_specs=P(None, "prow", None, None),
        check_vma=False,
    )
```

```python
import functools

import jax
import jax.numpy as jnp
from jax import lax
from jax.experimental import pallas as pl
from jax.experimental.pallas import tpu as pltpu
from jax.sharding import PartitionSpec as P

MESH = pl.DeviceIdType.MESH
NT = (((1,), (1,)), ((), ()))


def dot_nt(lhs, rhs):
    return lax.dot_general(lhs, rhs, NT, preferred_element_type=jnp.float32)


def kernel(
    n, nz, cols, rows,
    tiles, inverse, demand, out,
    gathered, diag, diag_split, asked, base, partial, sol, sol_split, sol_far, contrib, result, pick,
    own_sem, own_send, right_send, right_recv, left_send, left_recv,
    ask_own, ask_rsend, ask_rrecv, ask_lsend, ask_lrecv,
    diag_sem, base_send, base_recv, part_send, part_recv,
    far_send, far_recv, out_send, out_recv, swap_send, swap_recv,
):
    n2, hops = n // 2, nz // 2
    w = lax.axis_index("prow")
    q = lax.axis_index("pcol")
    z, c = q // 2, q % 2
    other = q + 1 - 2 * c
    right = lax.rem(z + 1, nz) * 2 + c
    left = lax.rem(z + nz - 1, nz) * 2 + c
    low = w < n2
    j = jnp.where(low, w, n - 1 - w)
    far = n - 1 - w
    count = jnp.where(low, n2, n2 - 1)
    shared = jnp.where(low, n2 - j, n2 - 1 - j)
    first = jnp.where(low, j + 1, j + 2)
    half = gathered.shape[1] * rows

    def remote(src, dst, send, recv, device):
        return pltpu.make_async_remote_copy(
            src_ref=src, dst_ref=dst, send_sem=send, recv_sem=recv,
            device_id=device, device_id_type=MESH,
        )

    def row_of(k):
        return jnp.where(k < shared, first + 2 * k, jnp.where(low, n2, n2 + 1) + k)

    def is_moved(k):
        return jnp.logical_and(jnp.logical_not(low), k < shared)

    def local_tile(k):
        return pltpu.make_async_copy(tiles.at[row_of(k)], gathered.at[k, z], own_sem.at[k])

    def moved_tile(k, row):
        return remote(tiles.at[row], gathered.at[k, z], own_send.at[k], own_sem.at[k], (far, q))

    def ring_right(k, h):
        o = lax.rem(z - h + nz, nz)
        return remote(gathered.at[k, o], gathered.at[k, o], right_send.at[k, h], right_recv.at[k, h], (w, right))

    def ring_left(k, h):
        o = lax.rem(z + h, nz)
        return remote(gathered.at[k, o], gathered.at[k, o], left_send.at[k, h], left_recv.at[k, h], (w, left))

    def ring_right_in(k, h):
        o = lax.rem(z - h - 1 + nz, nz)
        return remote(gathered.at[k, o], gathered.at[k, o], right_send.at[k, h], right_recv.at[k, h], (w, right))

    def ring_left_in(k, h):
        o = lax.rem(z + h + 1, nz)
        return remote(gathered.at[k, o], gathered.at[k, o], left_send.at[k, h], left_recv.at[k, h], (w, left))

    def ask_right(h):
        o = lax.rem(z - h + nz, nz)
        return remote(asked.at[o], asked.at[o], ask_rsend.at[h], ask_rrecv.at[h], (w, right))

    def ask_left(h):
        o = lax.rem(z + h, nz)
        return remote(asked.at[o], asked.at[o], ask_lsend.at[h], ask_lrecv.at[h], (w, left))

    def ask_right_in(h):
        o = lax.rem(z - h - 1 + nz, nz)
        return remote(asked.at[o], asked.at[o], ask_rsend.at[h], ask_rrecv.at[h], (w, right))

    def ask_left_in(h):
        o = lax.rem(z + h + 1, nz)
        return remote(asked.at[o], asked.at[o], ask_lsend.at[h], ask_lrecv.at[h], (w, left))

    base_copy = remote(base.at[c], base.at[c], base_send, base_recv, (w, other))
    base_in = remote(base.at[1 - c], base.at[1 - c], base_send, base_recv, (w, other))
    far_copy = remote(sol, sol_far, far_send, far_recv, (far, q))
    diag_copy = pltpu.make_async_copy(inverse, diag, diag_sem)
    ask_copy = pltpu.make_async_copy(demand.at[w], asked.at[z], ask_own)

    def part_copy(k, i, col, core):
        return remote(contrib.at[k], partial.at[col, c], part_send.at[k, core], part_recv.at[col, c], (i, 2 * z + core))

    def part_in(col, core):
        return remote(contrib.at[0], partial.at[col, core], part_send.at[0, 0], part_recv.at[col, core], (w, other))

    ask_copy.start()
    for k in range(n2):
        @pl.when(jnp.logical_and(k < count, jnp.logical_not(is_moved(k))))
        def _():
            local_tile(k).start()
    diag_copy.start()

    barrier = pltpu.get_barrier_semaphore()
    me = 2 * w + c

    def greet_plane(d, carry):
        t = lax.rem(me + d, 2 * n)
        pl.semaphore_signal(barrier, inc=1, device_id=(t // 2, 2 * z + t % 2), device_id_type=MESH)
        return carry

    def greet_ring(d, carry):
        t = lax.rem(z + d, nz)
        pl.semaphore_signal(barrier, inc=1, device_id=(w, 2 * t + c), device_id_type=MESH)
        return carry

    lax.fori_loop(1, 2 * n, greet_plane, 0)
    lax.fori_loop(1, nz, greet_ring, 0)
    pl.semaphore_wait(barrier, 2 * n - 1 + nz - 1)

    def gives(k):
        return jnp.logical_and(low, k < n2 - 1 - j)

    for k in range(n2 - 1):
        @pl.when(gives(k))
        def _():
            moved_tile(k, w + 2 + 2 * k).start()
    ask_copy.wait()

    def solve(i):
        @pl.when(i == 0)
        def _():
            diag_split_now()

        base_in.wait_recv()

        def add(col, acc):
            a, b = acc
            part_in(col, 0).wait_recv()
            part_in(col, 1).wait_recv()
            return a + partial[col, 0].astype(jnp.float32), b + partial[col, 1].astype(jnp.float32)

        zero = jnp.zeros((cols, half), jnp.float32)
        a, b = lax.fori_loop(0, i, add, (zero, zero))
        a = (base[0].astype(jnp.float32) - a).astype(jnp.bfloat16)
        b = (base[1].astype(jnp.float32) - b).astype(jnp.bfloat16)
        y = (dot_nt(a, diag_split[0]) + dot_nt(b, diag_split[1])).astype(jnp.bfloat16)
        sol[...] = y
        sol_split[0] = y[:, :half]
        sol_split[1] = y[:, half:]

        @pl.when(jnp.logical_and(i > 0, i < n - 1))
        def _():
            apply(i + 1, jnp.where(low, 0, i - n2), False)

        @pl.when(w < n2 - 1)
        def _():
            far_copy.start()

    def diag_split_now():
        diag_copy.wait()
        span, lane = 8 * rows, 4 * rows
        m = lax.broadcasted_iota(jnp.int32, (2 * rows, rows), 0)
        t = lax.broadcasted_iota(jnp.int32, (2 * rows, rows), 1)
        pick[...] = jnp.zeros_like(pick)
        for core in range(2):
            unit = (m == t + core * rows).astype(jnp.bfloat16)
            for b in range(4):
                lo = core * lane + b * rows
                pick[2 * rows * b:2 * rows * (b + 1), lo:lo + rows] = unit
        for u in range(diag.shape[1] // span):
            moved = jnp.dot(
                diag[:, u * span:(u + 1) * span], pick[...], preferred_element_type=jnp.float32
            ).astype(jnp.bfloat16)
            diag_split[0, :, u * lane:(u + 1) * lane] = moved[:, :lane]
            diag_split[1, :, u * lane:(u + 1) * lane] = moved[:, lane:]

    def apply(i, k, use_far):
        if use_far is False:
            col, y = w, sol[...]
        else:
            col = jnp.where(use_far, far, w)

            @pl.when(jnp.logical_and(use_far, k == 0))
            def _():
                far_copy.wait_recv()

            y = jnp.where(use_far, sol_far[...], sol[...])
        tile = gathered[k].reshape(half, gathered.shape[3])
        contrib[k] = dot_nt(y, tile).astype(jnp.bfloat16)
        part_copy(k, i, col, 0).start()
        part_copy(k, i, col, 1).start()

    def row_step(i):
        shared_end = first + 2 * (shared - 1)
        off = i - first
        near = jnp.logical_and(
            jnp.logical_and(off >= 0, i <= shared_end), lax.rem(off + 2 * n, 2) == 0
        )
        late = i > jnp.where(low, n - 1 - j, w)
        k = jnp.where(near, off // 2, i - jnp.where(low, n2, n2 + 1))
        k = jnp.where(jnp.logical_or(near, late), k, 0)

        done = jnp.logical_and(i == w + 1, w > 0)

        @pl.when(jnp.logical_and(jnp.logical_or(near, late), jnp.logical_not(done)))
        def _():
            apply(i, k, is_moved(k))

        @pl.when(i == w)
        def _():
            solve(i)

    def ring_slot(t):
        for m in range(hops // 2, -1, -1):
            k = t // 2 - m
            h = t % 2 + 2 * m
            live = jnp.logical_and(jnp.logical_and(k >= 0, k < count), h <= hops)

            @pl.when(jnp.logical_and(live, h == 0))
            def _():
                @pl.when(is_moved(k))
                def _():
                    moved_tile(k, 0).wait_recv()

                @pl.when(jnp.logical_not(is_moved(k)))
                def _():
                    local_tile(k).wait()

                ring_right(k, 0).start()
                ring_left(k, 0).start()

            @pl.when(jnp.logical_and(live, jnp.logical_and(h > 0, h < hops)))
            def _():
                ring_right_in(k, h - 1).wait_recv()
                ring_right(k, h).start()
                ring_left_in(k, h - 1).wait_recv()

                @pl.when(h < hops - 1)
                def _():
                    ring_left(k, h).start()

            @pl.when(jnp.logical_and(live, h == hops))
            def _():
                ring_right_in(k, h - 1).wait_recv()

    def ask_slot(t):
        @pl.when(t == 0)
        def _():
            ask_right(0).start()
            ask_left(0).start()

        @pl.when(jnp.logical_and(t > 0, t < hops))
        def _():
            ask_right_in(t - 1).wait_recv()
            ask_right(t).start()
            ask_left_in(t - 1).wait_recv()

            @pl.when(t < hops - 1)
            def _():
                ask_left(t).start()

        @pl.when(t == hops - 1)
        def _():
            ask_right_in(t).wait_recv()
            wide = asked.shape[2]
            mine = (
                lax.broadcasted_iota(jnp.int32, (cols, wide), 1)
                == cols * z + lax.broadcasted_iota(jnp.int32, (cols, wide), 0)
            ).astype(jnp.bfloat16)
            base[c] = dot_nt(mine, asked[...].reshape(half, wide)).astype(jnp.bfloat16)
            base_copy.start()

        @pl.when(jnp.logical_and(t == 2, w > 0))
        def _():
            diag_split_now()

    def slot(t, carry):
        ask_slot(t)
        ring_slot(t)
        i = t - (hops - 1)

        @pl.when(i >= 0)
        def _():
            row_step(i)

        return carry

    lax.fori_loop(0, n - 1 + hops, slot, 0)

    def out_copy(d):
        t = lax.rem(z + d, nz)
        return remote(sol_split.at[c], result.at[c, z], out_send.at[d], out_recv.at[d], (w, 2 * t + c))

    def out_in(d):
        t = lax.rem(z - d + nz, nz)
        return remote(sol_split.at[c], result.at[c, t], out_send.at[d], out_recv.at[d], (w, 2 * t + c))

    for d in range(1, hops + 1):
        out_copy(hops + 1 - d).start()
        if hops + d < nz:
            out_copy(hops + d).start()
    result[c, z] = sol_split[c]
    for d in range(1, nz):
        out_in(d).wait_recv()
    swap = remote(result.at[c], result.at[c], swap_send, swap_recv, (w, other))
    swap.start()

    for k in range(n2 - 1):
        @pl.when(gives(k))
        def _():
            moved_tile(k, w + 2 + 2 * k).wait_send()
    for k in range(n2):
        @pl.when(k < count)
        def _():
            for h in range(hops):
                ring_right(k, h).wait_send()
            for h in range(hops - 1):
                ring_left(k, h).wait_send()
            part_copy(k, 0, 0, 0).wait_send()
            part_copy(k, 0, 0, 1).wait_send()
    for h in range(hops):
        ask_right(h).wait_send()
    for h in range(hops - 1):
        ask_left(h).wait_send()
    base_copy.wait_send()

    @pl.when(w < n2 - 1)
    def _():
        far_copy.wait_send()

    for d in range(1, nz):
        out_copy(d).wait_send()
    swap.wait_send()
    remote(result.at[1 - c], result.at[1 - c], swap_send, swap_recv, (w, other)).wait_recv()
    for s in range(2):
        out[:, s * half:(s + 1) * half] = result[s].reshape(nz * cols, half)


def on_device(factor_tiles, inverse_blocks, demand):
    n, rows, _, _, width = factor_tiles.shape
    nz = lax.axis_size("pcol") // 2
    wide = demand.shape[2]
    cols = wide // nz
    half = width // 2
    n2, hops = n // 2, nz // 2
    dma = pltpu.SemaphoreType.DMA
    out = pl.pallas_call(
        functools.partial(kernel, n, nz, cols, rows),
        out_shape=jax.ShapeDtypeStruct((wide, width), jnp.bfloat16),
        in_specs=[pl.BlockSpec(memory_space=pltpu.HBM)] * 3,
        out_specs=pl.BlockSpec(memory_space=pltpu.VMEM),
        scratch_shapes=[
            pltpu.VMEM((n2, nz, rows, width), jnp.bfloat16),
            pltpu.VMEM((width, width), jnp.bfloat16),
            pltpu.VMEM((2, width, half), jnp.bfloat16),
            pltpu.VMEM((nz, rows, wide), jnp.bfloat16),
            pltpu.VMEM((2, cols, half), jnp.bfloat16),
            pltpu.VMEM((n, 2, cols, half), jnp.bfloat16),
            pltpu.VMEM((cols, width), jnp.bfloat16),
            pltpu.VMEM((2, cols, half), jnp.bfloat16),
            pltpu.VMEM((cols, width), jnp.bfloat16),
            pltpu.VMEM((n2, cols, half), jnp.bfloat16),
            pltpu.VMEM((2, nz, cols, half), jnp.bfloat16),
            pltpu.VMEM((8 * rows, 8 * rows), jnp.bfloat16),
            dma((n2,)), dma((n2,)),
            dma((n2, hops)), dma((n2, hops)), dma((n2, hops - 1)), dma((n2, hops - 1)),
            dma, dma((hops,)), dma((hops,)), dma((hops - 1,)), dma((hops - 1,)),
            dma, dma, dma, dma((n2, 2)), dma((n, 2)),
            dma, dma, dma((nz,)), dma((nz,)), dma, dma,
        ],
        compiler_params=pltpu.CompilerParams(
            collective_id=0, has_side_effects=True, vmem_limit_bytes=48 * 1024 * 1024
        ),
    )(
        factor_tiles.reshape(n, rows, width),
        inverse_blocks.reshape(width, width),
        demand,
    )
    return out.T.reshape(1, 1, width, wide)


def solution(mesh):
    placed = (
        P(None, "pcol", None, "prow", None),
        P(None, "prow", None, None),
        P(None, "pcol", None),
    )
    return jax.shard_map(
        on_device,
        mesh=mesh,
        in_specs=placed,
        out_specs=P(None, "prow", None, None),
        check_vma=False,
    )
```

```python
import functools

import jax
import jax.numpy as jnp
from jax import lax
from jax.experimental import pallas as pl
from jax.experimental.pallas import tpu as pltpu
from jax.sharding import PartitionSpec as P

MESH = pl.DeviceIdType.MESH
NT = (((1,), (1,)), ((), ()))


def dot_nt(lhs, rhs):
    return lax.dot_general(lhs, rhs, NT, preferred_element_type=jnp.float32)


def kernel(
    n, nz, cols, rows,
    tiles, inverse, demand, out,
    gathered, diag, diag_split, asked, base, partial, sol, sol_split, sol_far, contrib, result, pick,
    own_sem, own_send, right_send, right_recv, left_send, left_recv,
    ask_own, ask_rsend, ask_rrecv, ask_lsend, ask_lrecv,
    diag_sem, base_send, base_recv, part_send, part_recv,
    far_send, far_recv, out_send, out_recv, swap_send, swap_recv,
):
    n2, hops = n // 2, nz // 2
    w = lax.axis_index("prow")
    q = lax.axis_index("pcol")
    z, c = q // 2, q % 2
    other = q + 1 - 2 * c
    turn = 1 - 2 * c

    def along(steps):
        return lax.rem(z + turn * steps + nz, nz)

    right = along(1) * 2 + c
    left = along(-1) * 2 + c
    low = w < n2
    j = jnp.where(low, w, n - 1 - w)
    far = n - 1 - w
    count = jnp.where(low, n2, n2 - 1)
    shared = jnp.where(low, n2 - j, n2 - 1 - j)
    first = jnp.where(low, j + 1, j + 2)
    half = gathered.shape[1] * rows

    def remote(src, dst, send, recv, device):
        return pltpu.make_async_remote_copy(
            src_ref=src, dst_ref=dst, send_sem=send, recv_sem=recv,
            device_id=device, device_id_type=MESH,
        )

    def row_of(k):
        return jnp.where(k < shared, first + 2 * k, jnp.where(low, n2, n2 + 1) + k)

    def is_moved(k):
        return jnp.logical_and(jnp.logical_not(low), k < shared)

    def local_tile(k):
        return pltpu.make_async_copy(tiles.at[row_of(k)], gathered.at[k, z], own_sem.at[k])

    def moved_tile(k, row):
        return remote(tiles.at[row], gathered.at[k, z], own_send.at[k], own_sem.at[k], (far, q))

    def ring_right(k, h):
        o = along(-h)
        return remote(gathered.at[k, o], gathered.at[k, o], right_send.at[k, h], right_recv.at[k, h], (w, right))

    def ring_left(k, h):
        o = along(h)
        return remote(gathered.at[k, o], gathered.at[k, o], left_send.at[k, h], left_recv.at[k, h], (w, left))

    def ring_right_in(k, h):
        o = along(-h - 1)
        return remote(gathered.at[k, o], gathered.at[k, o], right_send.at[k, h], right_recv.at[k, h], (w, right))

    def ring_left_in(k, h):
        o = along(h + 1)
        return remote(gathered.at[k, o], gathered.at[k, o], left_send.at[k, h], left_recv.at[k, h], (w, left))

    def ask_right(h):
        o = along(-h)
        return remote(asked.at[o], asked.at[o], ask_rsend.at[h], ask_rrecv.at[h], (w, right))

    def ask_left(h):
        o = along(h)
        return remote(asked.at[o], asked.at[o], ask_lsend.at[h], ask_lrecv.at[h], (w, left))

    def ask_right_in(h):
        o = along(-h - 1)
        return remote(asked.at[o], asked.at[o], ask_rsend.at[h], ask_rrecv.at[h], (w, right))

    def ask_left_in(h):
        o = along(h + 1)
        return remote(asked.at[o], asked.at[o], ask_lsend.at[h], ask_lrecv.at[h], (w, left))

    base_copy = remote(base.at[c], base.at[c], base_send, base_recv, (w, other))
    base_in = remote(base.at[1 - c], base.at[1 - c], base_send, base_recv, (w, other))
    far_copy = remote(sol, sol_far, far_send, far_recv, (far, q))
    diag_copy = pltpu.make_async_copy(inverse, diag, diag_sem)
    ask_copy = pltpu.make_async_copy(demand.at[w], asked.at[z], ask_own)

    def part_copy(k, i, col, core):
        return remote(contrib.at[k], partial.at[col, c], part_send.at[k, core], part_recv.at[col, c], (i, 2 * z + core))

    def part_in(col, core):
        return remote(contrib.at[0], partial.at[col, core], part_send.at[0, 0], part_recv.at[col, core], (w, other))

    ask_copy.start()
    for k in range(n2):
        @pl.when(jnp.logical_and(k < count, jnp.logical_not(is_moved(k))))
        def _():
            local_tile(k).start()
    diag_copy.start()

    barrier = pltpu.get_barrier_semaphore()
    me = 2 * w + c

    def greet_plane(d, carry):
        t = lax.rem(me + d, 2 * n)
        pl.semaphore_signal(barrier, inc=1, device_id=(t // 2, 2 * z + t % 2), device_id_type=MESH)
        return carry

    lax.fori_loop(1, 2 * n, greet_plane, 0)
    for side in (right, left):
        pl.semaphore_signal(barrier, inc=1, device_id=(w, side), device_id_type=MESH)
    diag_copy.wait()
    span, lane = 8 * rows, 4 * rows
    m = lax.broadcasted_iota(jnp.int32, (2 * rows, rows), 0)
    t = lax.broadcasted_iota(jnp.int32, (2 * rows, rows), 1)
    pick[...] = jnp.zeros_like(pick)
    for core in range(2):
        unit = (m == t + core * rows).astype(jnp.bfloat16)
        for b in range(4):
            lo = core * lane + b * rows
            pick[2 * rows * b:2 * rows * (b + 1), lo:lo + rows] = unit
    for u in range(diag.shape[1] // span):
        moved = jnp.dot(
            diag[:, u * span:(u + 1) * span], pick[...], preferred_element_type=jnp.float32
        ).astype(jnp.bfloat16)
        diag_split[0, :, u * lane:(u + 1) * lane] = moved[:, :lane]
        diag_split[1, :, u * lane:(u + 1) * lane] = moved[:, lane:]
    pl.semaphore_wait(barrier, 2 * n - 1 + 2)

    def gives(k):
        return jnp.logical_and(low, k < n2 - 1 - j)

    for k in range(n2 - 1):
        @pl.when(gives(k))
        def _():
            moved_tile(k, w + 2 + 2 * k).start()
    ask_copy.wait()

    def solve(i):
        base_in.wait_recv()

        def add(col, acc):
            a, b = acc
            part_in(col, 0).wait_recv()
            part_in(col, 1).wait_recv()
            return a + partial[col, 0].astype(jnp.float32), b + partial[col, 1].astype(jnp.float32)

        zero = jnp.zeros((cols, half), jnp.float32)
        a, b = lax.fori_loop(0, i, add, (zero, zero))
        a = (base[0].astype(jnp.float32) - a).astype(jnp.bfloat16)
        b = (base[1].astype(jnp.float32) - b).astype(jnp.bfloat16)
        y = (dot_nt(a, diag_split[0]) + dot_nt(b, diag_split[1])).astype(jnp.bfloat16)
        sol[...] = y
        sol_split[0] = y[:, :half]
        sol_split[1] = y[:, half:]

        @pl.when(jnp.logical_and(i > 0, i < n - 1))
        def _():
            apply(i + 1, jnp.where(low, 0, i - n2), False)

        @pl.when(w < n2 - 1)
        def _():
            far_copy.start()

    def apply(i, k, use_far):
        if use_far is False:
            col, y = w, sol[...]
        else:
            col = jnp.where(use_far, far, w)

            @pl.when(jnp.logical_and(use_far, k == 0))
            def _():
                far_copy.wait_recv()

            y = jnp.where(use_far, sol_far[...], sol[...])
        ring_right_in(k, hops - 1).wait_recv()
        tile = gathered[k].reshape(half, gathered.shape[3])
        contrib[k] = dot_nt(y, tile).astype(jnp.bfloat16)
        part_copy(k, i, col, 0).start()
        part_copy(k, i, col, 1).start()

    def row_step(i):
        shared_end = first + 2 * (shared - 1)
        off = i - first
        near = jnp.logical_and(
            jnp.logical_and(off >= 0, i <= shared_end), lax.rem(off + 2 * n, 2) == 0
        )
        late = i > jnp.where(low, n - 1 - j, w)
        k = jnp.where(near, off // 2, i - jnp.where(low, n2, n2 + 1))
        k = jnp.where(jnp.logical_or(near, late), k, 0)

        done = jnp.logical_and(i == w + 1, w > 0)

        @pl.when(jnp.logical_and(jnp.logical_or(near, late), jnp.logical_not(done)))
        def _():
            apply(i, k, is_moved(k))

        @pl.when(i == w)
        def _():
            solve(i)

    def ring_slot(u, parity):
        for m in range(hops // 2, -1, -1):
            h = parity + 2 * m
            if h >= hops:
                continue
            k = u - m

            @pl.when(jnp.logical_and(k >= 0, k < count))
            def _():
                if h == 0:
                    @pl.when(is_moved(k))
                    def _():
                        moved_tile(k, 0).wait_recv()

                    @pl.when(jnp.logical_not(is_moved(k)))
                    def _():
                        local_tile(k).wait()
                else:
                    ring_right_in(k, h - 1).wait_recv()
                ring_right(k, h).start()
                if h > 0:
                    ring_left_in(k, h - 1).wait_recv()
                if h < hops - 1:
                    ring_left(k, h).start()

    def ask_slot(t):
        @pl.when(t == 0)
        def _():
            ask_right(0).start()
            ask_left(0).start()

        @pl.when(jnp.logical_and(t > 0, t < hops))
        def _():
            ask_right_in(t - 1).wait_recv()
            ask_right(t).start()
            ask_left_in(t - 1).wait_recv()

            @pl.when(t < hops - 1)
            def _():
                ask_left(t).start()

        @pl.when(t == hops - 1)
        def _():
            ask_right_in(t).wait_recv()
            wide = asked.shape[2]
            mine = (
                lax.broadcasted_iota(jnp.int32, (cols, wide), 1)
                == cols * z + lax.broadcasted_iota(jnp.int32, (cols, wide), 0)
            ).astype(jnp.bfloat16)
            base[c] = dot_nt(mine, asked[...].reshape(half, wide)).astype(jnp.bfloat16)
            base_copy.start()

    def slot_pair(u, carry):
        for parity in range(2):
            t = 2 * u + parity

            @pl.when(t < hops)
            def _():
                ask_slot(t)

            ring_slot(u, parity)
            i = t - (hops - 1)

            @pl.when(jnp.logical_and(i >= 0, i < n))
            def _():
                row_step(i)

        return carry

    lax.fori_loop(0, (n + hops) // 2, slot_pair, 0)

    def out_copy(d):
        t = lax.rem(z + d, nz)
        return remote(sol_split.at[c], result.at[c, z], out_send.at[d], out_recv.at[d], (w, 2 * t + c))

    def out_in(d):
        t = lax.rem(z - d + nz, nz)
        return remote(sol_split.at[c], result.at[c, t], out_send.at[d], out_recv.at[d], (w, 2 * t + c))

    for d in range(1, hops + 1):
        out_copy(hops + 1 - d).start()
        if hops + d < nz:
            out_copy(hops + d).start()
    result[c, z] = sol_split[c]
    for d in range(1, nz):
        out_in(d).wait_recv()
    swap = remote(result.at[c], result.at[c], swap_send, swap_recv, (w, other))
    swap.start()

    for k in range(n2 - 1):
        @pl.when(gives(k))
        def _():
            moved_tile(k, w + 2 + 2 * k).wait_send()
    for k in range(n2):
        @pl.when(k < count)
        def _():
            for h in range(hops):
                ring_right(k, h).wait_send()
            for h in range(hops - 1):
                ring_left(k, h).wait_send()
            part_copy(k, 0, 0, 0).wait_send()
            part_copy(k, 0, 0, 1).wait_send()
    for h in range(hops):
        ask_right(h).wait_send()
    for h in range(hops - 1):
        ask_left(h).wait_send()
    base_copy.wait_send()

    @pl.when(w < n2 - 1)
    def _():
        far_copy.wait_send()

    for d in range(1, nz):
        out_copy(d).wait_send()
    swap.wait_send()
    remote(result.at[1 - c], result.at[1 - c], swap_send, swap_recv, (w, other)).wait_recv()
    for s in range(2):
        out[:, s * half:(s + 1) * half] = result[s].reshape(nz * cols, half)


def on_device(factor_tiles, inverse_blocks, demand):
    n, rows, _, _, width = factor_tiles.shape
    nz = lax.axis_size("pcol") // 2
    wide = demand.shape[2]
    cols = wide // nz
    half = width // 2
    n2, hops = n // 2, nz // 2
    dma = pltpu.SemaphoreType.DMA
    out = pl.pallas_call(
        functools.partial(kernel, n, nz, cols, rows),
        out_shape=jax.ShapeDtypeStruct((wide, width), jnp.bfloat16),
        in_specs=[pl.BlockSpec(memory_space=pltpu.HBM)] * 3,
        out_specs=pl.BlockSpec(memory_space=pltpu.VMEM),
        scratch_shapes=[
            pltpu.VMEM((n2, nz, rows, width), jnp.bfloat16),
            pltpu.VMEM((width, width), jnp.bfloat16),
            pltpu.VMEM((2, width, half), jnp.bfloat16),
            pltpu.VMEM((nz, rows, wide), jnp.bfloat16),
            pltpu.VMEM((2, cols, half), jnp.bfloat16),
            pltpu.VMEM((n, 2, cols, half), jnp.bfloat16),
            pltpu.VMEM((cols, width), jnp.bfloat16),
            pltpu.VMEM((2, cols, half), jnp.bfloat16),
            pltpu.VMEM((cols, width), jnp.bfloat16),
            pltpu.VMEM((n2, cols, half), jnp.bfloat16),
            pltpu.VMEM((2, nz, cols, half), jnp.bfloat16),
            pltpu.VMEM((8 * rows, 8 * rows), jnp.bfloat16),
            dma((n2,)), dma((n2,)),
            dma((n2, hops)), dma((n2, hops)), dma((n2, hops - 1)), dma((n2, hops - 1)),
            dma, dma((hops,)), dma((hops,)), dma((hops - 1,)), dma((hops - 1,)),
            dma, dma, dma, dma((n2, 2)), dma((n, 2)),
            dma, dma, dma((nz,)), dma((nz,)), dma, dma,
        ],
        compiler_params=pltpu.CompilerParams(
            collective_id=0, has_side_effects=True
        ),
    )(
        factor_tiles.reshape(n, rows, width),
        inverse_blocks.reshape(width, width),
        demand,
    )
    return out.T.reshape(1, 1, width, wide)


def solution(mesh):
    placed = (
        P(None, "pcol", None, "prow", None),
        P(None, "prow", None, None),
        P(None, "pcol", None),
    )
    return jax.shard_map(
        on_device,
        mesh=mesh,
        in_specs=placed,
        out_specs=P(None, "prow", None, None),
        check_vma=False,
    )
```

```python
import functools

import jax
import jax.numpy as jnp
from jax import lax
from jax.experimental import pallas as pl
from jax.experimental.pallas import tpu as pltpu
from jax.sharding import PartitionSpec as P

MESH = pl.DeviceIdType.MESH
NT = (((1,), (1,)), ((), ()))


def dot_nt(lhs, rhs):
    return lax.dot_general(lhs, rhs, NT, preferred_element_type=jnp.float32)


def kernel(
    n, nz, cols, rows,
    tiles, inverse, demand, out,
    gathered, diag, diag_split, asked, base, partial, sol, sol_split, sol_far, contrib, result, pick,
    own_sem, own_send, right_send, right_recv, left_send, left_recv,
    ask_own, ask_rsend, ask_rrecv, ask_lsend, ask_lrecv,
    diag_sem, base_send, base_recv, part_send, part_recv,
    far_send, far_recv, out_send, out_recv, swap_send, swap_recv,
):
    n2, hops = n // 2, nz // 2
    w = lax.axis_index("prow")
    q = lax.axis_index("pcol")
    z, c = q // 2, q % 2
    other = q + 1 - 2 * c
    turn = 1 - 2 * c

    def along(steps):
        return lax.rem(z + turn * steps + nz, nz)

    right = along(1) * 2 + c
    left = along(-1) * 2 + c
    low = w < n2
    j = jnp.where(low, w, n - 1 - w)
    far = n - 1 - w
    count = jnp.where(low, n2, n2 - 1)
    shared = jnp.where(low, n2 - j, n2 - 1 - j)
    span_j = n - 1 - 2 * j
    half = gathered.shape[1] * rows

    def remote(src, dst, send, recv, device):
        return pltpu.make_async_remote_copy(
            src_ref=src, dst_ref=dst, send_sem=send, recv_sem=recv,
            device_id=device, device_id_type=MESH,
        )

    def row_of(k):
        own = jnp.where(k == 0, 1, jnp.where(k == shared - 1, span_j, 2 * k))
        moved = jnp.where(k == shared - 1, span_j - 1, 2 * k + 3)
        near = j + jnp.where(low, own, moved)
        return jnp.where(k < shared, near, jnp.where(low, n2, n2 + 1) + k)

    def is_moved(k):
        return jnp.logical_and(jnp.logical_not(low), k < shared)

    def local_tile(k):
        return pltpu.make_async_copy(tiles.at[row_of(k)], gathered.at[k, z], own_sem.at[k])

    def moved_tile(k, row):
        return remote(tiles.at[row], gathered.at[k, z], own_send.at[k], own_sem.at[k], (far, q))

    def ring_right(k, h):
        o = along(-h)
        return remote(gathered.at[k, o], gathered.at[k, o], right_send.at[k, h], right_recv.at[k, h], (w, right))

    def ring_left(k, h):
        o = along(h)
        return remote(gathered.at[k, o], gathered.at[k, o], left_send.at[k, h], left_recv.at[k, h], (w, left))

    def ring_right_in(k, h):
        o = along(-h - 1)
        return remote(gathered.at[k, o], gathered.at[k, o], right_send.at[k, h], right_recv.at[k, h], (w, right))

    def ring_left_in(k, h):
        o = along(h + 1)
        return remote(gathered.at[k, o], gathered.at[k, o], left_send.at[k, h], left_recv.at[k, h], (w, left))

    def ask_right(h):
        o = along(-h)
        return remote(asked.at[o], asked.at[o], ask_rsend.at[h], ask_rrecv.at[h], (w, right))

    def ask_left(h):
        o = along(h)
        return remote(asked.at[o], asked.at[o], ask_lsend.at[h], ask_lrecv.at[h], (w, left))

    def ask_right_in(h):
        o = along(-h - 1)
        return remote(asked.at[o], asked.at[o], ask_rsend.at[h], ask_rrecv.at[h], (w, right))

    def ask_left_in(h):
        o = along(h + 1)
        return remote(asked.at[o], asked.at[o], ask_lsend.at[h], ask_lrecv.at[h], (w, left))

    base_copy = remote(base.at[c], base.at[c], base_send, base_recv, (w, other))
    base_in = remote(base.at[1 - c], base.at[1 - c], base_send, base_recv, (w, other))
    far_copy = remote(sol, sol_far, far_send, far_recv, (far, q))
    diag_copy = pltpu.make_async_copy(inverse, diag, diag_sem)
    ask_copy = pltpu.make_async_copy(demand.at[w], asked.at[z], ask_own)

    def part_copy(k, i, col, core):
        return remote(contrib.at[k], partial.at[col, c], part_send.at[k, core], part_recv.at[col, c], (i, 2 * z + core))

    def part_in(col, core):
        return remote(contrib.at[0], partial.at[col, core], part_send.at[0, 0], part_recv.at[col, core], (w, other))

    ask_copy.start()
    for k in range(n2):
        @pl.when(jnp.logical_and(k < count, jnp.logical_not(is_moved(k))))
        def _():
            local_tile(k).start()
    diag_copy.start()

    barrier = pltpu.get_barrier_semaphore()
    me = 2 * w + c

    def greet_plane(d, carry):
        t = lax.rem(me + d, 2 * n)
        pl.semaphore_signal(barrier, inc=1, device_id=(t // 2, 2 * z + t % 2), device_id_type=MESH)
        return carry

    lax.fori_loop(1, 2 * n, greet_plane, 0)
    for side in (right, left):
        pl.semaphore_signal(barrier, inc=1, device_id=(w, side), device_id_type=MESH)
    diag_copy.wait()
    span, lane = 8 * rows, 4 * rows
    m = lax.broadcasted_iota(jnp.int32, (2 * rows, rows), 0)
    t = lax.broadcasted_iota(jnp.int32, (2 * rows, rows), 1)
    pick[...] = jnp.zeros_like(pick)
    for core in range(2):
        unit = (m == t + core * rows).astype(jnp.bfloat16)
        for b in range(4):
            lo = core * lane + b * rows
            pick[2 * rows * b:2 * rows * (b + 1), lo:lo + rows] = unit
    for u in range(diag.shape[1] // span):
        moved = jnp.dot(
            diag[:, u * span:(u + 1) * span], pick[...], preferred_element_type=jnp.float32
        ).astype(jnp.bfloat16)
        diag_split[0, :, u * lane:(u + 1) * lane] = moved[:, :lane]
        diag_split[1, :, u * lane:(u + 1) * lane] = moved[:, lane:]
    pl.semaphore_wait(barrier, 2 * n - 1 + 2)

    def gives(k):
        return jnp.logical_and(low, k < n2 - 1 - j)

    for k in range(n2 - 1):
        @pl.when(gives(k))
        def _():
            moved_tile(k, w + jnp.where(k == n2 - 2 - j, span_j - 1, 2 * k + 3)).start()
    ask_copy.wait()

    def solve(i):
        base_in.wait_recv()

        def add(col, acc):
            a, b = acc
            part_in(col, 0).wait_recv()
            part_in(col, 1).wait_recv()
            return a + partial[col, 0].astype(jnp.float32), b + partial[col, 1].astype(jnp.float32)

        zero = jnp.zeros((cols, half), jnp.float32)
        a, b = lax.fori_loop(0, i, add, (zero, zero))
        a = (base[0].astype(jnp.float32) - a).astype(jnp.bfloat16)
        b = (base[1].astype(jnp.float32) - b).astype(jnp.bfloat16)
        y = (dot_nt(a, diag_split[0]) + dot_nt(b, diag_split[1])).astype(jnp.bfloat16)
        sol[...] = y
        sol_split[0] = y[:, :half]
        sol_split[1] = y[:, half:]

        @pl.when(w < n2 - 1)
        def _():
            far_copy.start()

    def apply(k, use_far):
        col = jnp.where(use_far, far, w)
        y = jnp.where(use_far, sol_far[...], sol[...])
        ring_right_in(k, hops - 1).wait_recv()
        tile = gathered[k].reshape(half, gathered.shape[3])
        contrib[k] = dot_nt(y, tile).astype(jnp.bfloat16)
        row = row_of(k)
        part_copy(k, row, col, 0).start()
        part_copy(k, row, col, 1).start()

    def row_step(i):
        last = i // 2
        own_event = i == w
        far_event = jnp.logical_and(jnp.logical_not(low), jnp.logical_and(i == j + 2, shared > 0))
        since = jnp.where(is_moved(last), j + 2, w)
        ready = jnp.logical_and(lax.rem(i, 2) == 0, jnp.logical_and(last < count, i > since))
        start = jnp.where(own_event, jnp.where(low, 0, shared), jnp.where(far_event, 0, last))
        stop = jnp.where(
            own_event,
            jnp.minimum(last, count - 1),
            jnp.where(far_event, jnp.minimum(last, shared - 1), jnp.where(ready, last, start - 1)),
        )

        @pl.when(own_event)
        def _():
            solve(i)

        @pl.when(far_event)
        def _():
            far_copy.wait_recv()

        use_far = is_moved(start)

        def step(k, carry):
            apply(k, use_far)
            return carry

        lax.fori_loop(start, stop + 1, step, 0)

    def ring_slot(u, parity):
        for m in range(hops // 2, -1, -1):
            h = parity + 2 * m
            if h >= hops:
                continue
            k = u - m

            @pl.when(jnp.logical_and(k >= 0, k < count))
            def _():
                if h == 0:
                    @pl.when(is_moved(k))
                    def _():
                        moved_tile(k, 0).wait_recv()

                    @pl.when(jnp.logical_not(is_moved(k)))
                    def _():
                        local_tile(k).wait()
                else:
                    ring_right_in(k, h - 1).wait_recv()
                ring_right(k, h).start()
                if h > 0:
                    ring_left_in(k, h - 1).wait_recv()
                if h < hops - 1:
                    ring_left(k, h).start()

    def ask_slot(t):
        @pl.when(t == 0)
        def _():
            ask_right(0).start()
            ask_left(0).start()

        @pl.when(jnp.logical_and(t > 0, t < hops))
        def _():
            ask_right_in(t - 1).wait_recv()
            ask_right(t).start()
            ask_left_in(t - 1).wait_recv()

            @pl.when(t < hops - 1)
            def _():
                ask_left(t).start()

        @pl.when(t == hops - 1)
        def _():
            ask_right_in(t).wait_recv()
            wide = asked.shape[2]
            mine = (
                lax.broadcasted_iota(jnp.int32, (cols, wide), 1)
                == cols * z + lax.broadcasted_iota(jnp.int32, (cols, wide), 0)
            ).astype(jnp.bfloat16)
            base[c] = dot_nt(mine, asked[...].reshape(half, wide)).astype(jnp.bfloat16)
            base_copy.start()

    def slot_pair(u, carry):
        for parity in range(2):
            t = 2 * u + parity

            @pl.when(t < hops)
            def _():
                ask_slot(t)

            ring_slot(u, parity)
            i = t - (hops - 1)

            @pl.when(jnp.logical_and(i >= 0, i < n))
            def _():
                row_step(i)

        return carry

    lax.fori_loop(0, (n + hops) // 2, slot_pair, 0)

    def out_copy(d):
        t = lax.rem(z + d, nz)
        return remote(sol_split.at[c], result.at[c, z], out_send.at[d], out_recv.at[d], (w, 2 * t + c))

    def out_in(d):
        t = lax.rem(z - d + nz, nz)
        return remote(sol_split.at[c], result.at[c, t], out_send.at[d], out_recv.at[d], (w, 2 * t + c))

    for d in range(1, hops + 1):
        out_copy(hops + 1 - d).start()
        if hops + d < nz:
            out_copy(hops + d).start()
    result[c, z] = sol_split[c]
    for d in range(1, nz):
        out_in(d).wait_recv()
    swap = remote(result.at[c], result.at[c], swap_send, swap_recv, (w, other))
    swap.start()

    for k in range(n2 - 1):
        @pl.when(gives(k))
        def _():
            moved_tile(k, w + jnp.where(k == n2 - 2 - j, span_j - 1, 2 * k + 3)).wait_send()
    for k in range(n2):
        @pl.when(k < count)
        def _():
            for h in range(hops):
                ring_right(k, h).wait_send()
            for h in range(hops - 1):
                ring_left(k, h).wait_send()
            part_copy(k, 0, 0, 0).wait_send()
            part_copy(k, 0, 0, 1).wait_send()
    for h in range(hops):
        ask_right(h).wait_send()
    for h in range(hops - 1):
        ask_left(h).wait_send()
    base_copy.wait_send()

    @pl.when(w < n2 - 1)
    def _():
        far_copy.wait_send()

    for d in range(1, nz):
        out_copy(d).wait_send()
    swap.wait_send()
    remote(result.at[1 - c], result.at[1 - c], swap_send, swap_recv, (w, other)).wait_recv()
    for s in range(2):
        out[:, s * half:(s + 1) * half] = result[s].reshape(nz * cols, half)


def on_device(factor_tiles, inverse_blocks, demand):
    n, rows, _, _, width = factor_tiles.shape
    nz = lax.axis_size("pcol") // 2
    wide = demand.shape[2]
    cols = wide // nz
    half = width // 2
    n2, hops = n // 2, nz // 2
    dma = pltpu.SemaphoreType.DMA
    out = pl.pallas_call(
        functools.partial(kernel, n, nz, cols, rows),
        out_shape=jax.ShapeDtypeStruct((wide, width), jnp.bfloat16),
        in_specs=[pl.BlockSpec(memory_space=pltpu.HBM)] * 3,
        out_specs=pl.BlockSpec(memory_space=pltpu.VMEM),
        scratch_shapes=[
            pltpu.VMEM((n2, nz, rows, width), jnp.bfloat16),
            pltpu.VMEM((width, width), jnp.bfloat16),
            pltpu.VMEM((2, width, half), jnp.bfloat16),
            pltpu.VMEM((nz, rows, wide), jnp.bfloat16),
            pltpu.VMEM((2, cols, half), jnp.bfloat16),
            pltpu.VMEM((n, 2, cols, half), jnp.bfloat16),
            pltpu.VMEM((cols, width), jnp.bfloat16),
            pltpu.VMEM((2, cols, half), jnp.bfloat16),
            pltpu.VMEM((cols, width), jnp.bfloat16),
            pltpu.VMEM((n2, cols, half), jnp.bfloat16),
            pltpu.VMEM((2, nz, cols, half), jnp.bfloat16),
            pltpu.VMEM((8 * rows, 8 * rows), jnp.bfloat16),
            dma((n2,)), dma((n2,)),
            dma((n2, hops)), dma((n2, hops)), dma((n2, hops - 1)), dma((n2, hops - 1)),
            dma, dma((hops,)), dma((hops,)), dma((hops - 1,)), dma((hops - 1,)),
            dma, dma, dma, dma((n2, 2)), dma((n, 2)),
            dma, dma, dma((nz,)), dma((nz,)), dma, dma,
        ],
        compiler_params=pltpu.CompilerParams(
            collective_id=0, has_side_effects=True
        ),
    )(
        factor_tiles.reshape(n, rows, width),
        inverse_blocks.reshape(width, width),
        demand,
    )
    return out.T.reshape(1, 1, width, wide)


def solution(mesh):
    placed = (
        P(None, "pcol", None, "prow", None),
        P(None, "prow", None, None),
        P(None, "pcol", None),
    )
    return jax.shard_map(
        on_device,
        mesh=mesh,
        in_specs=placed,
        out_specs=P(None, "prow", None, None),
        check_vma=False,
    )
```

```python
import functools

import jax
import jax.numpy as jnp
from jax import lax
from jax.experimental import pallas as pl
from jax.experimental.pallas import tpu as pltpu
from jax.sharding import PartitionSpec as P

MESH = pl.DeviceIdType.MESH
NT = (((1,), (1,)), ((), ()))


def dot_nt(lhs, rhs):
    return lax.dot_general(lhs, rhs, NT, preferred_element_type=jnp.float32)


def kernel(
    n, nz, cols, rows,
    tiles, inverse, demand, out,
    gathered, diag, diag_split, asked, base, partial, sol, sol_split, sol_far, contrib, result, pick,
    own_sem, own_send, right_send, right_recv, left_send, left_recv,
    ask_own, ask_rsend, ask_rrecv, ask_lsend, ask_lrecv,
    diag_sem, base_send, base_recv, part_send, part_recv,
    far_send, far_recv, out_send, out_recv, swap_send, swap_recv,
):
    n2, hops = n // 2, nz // 2
    w = lax.axis_index("prow")
    q = lax.axis_index("pcol")
    z, c = q // 2, q % 2
    other = q + 1 - 2 * c
    turn = 1 - 2 * c

    def along(steps):
        return lax.rem(z + turn * steps + nz, nz)

    right = along(1) * 2 + c
    left = along(-1) * 2 + c
    low = w < n2
    j = jnp.where(low, w, n - 1 - w)
    far = n - 1 - w
    count = jnp.where(low, n2, n2 - 1)
    shared = jnp.where(low, n2 - j, n2 - 1 - j)
    span_j = n - 1 - 2 * j
    half = gathered.shape[1] * rows

    def remote(src, dst, send, recv, device):
        return pltpu.make_async_remote_copy(
            src_ref=src, dst_ref=dst, send_sem=send, recv_sem=recv,
            device_id=device, device_id_type=MESH,
        )

    def row_of(k):
        own = jnp.where(k == 0, 1, jnp.where(k == shared - 1, span_j, 2 * k))
        moved = jnp.where(k == shared - 1, span_j - 1, 2 * k + 3)
        near = j + jnp.where(low, own, moved)
        return jnp.where(k < shared, near, jnp.where(low, n2, n2 + 1) + k)

    def is_moved(k):
        return jnp.logical_and(jnp.logical_not(low), k < shared)

    def local_tile(k):
        return pltpu.make_async_copy(tiles.at[row_of(k)], gathered.at[k, z], own_sem.at[k])

    def moved_tile(k, row):
        return remote(tiles.at[row], gathered.at[k, z], own_send.at[k], own_sem.at[k], (far, q))

    def ring_right(k, h):
        o = along(-h)
        return remote(gathered.at[k, o], gathered.at[k, o], right_send.at[k, h], right_recv.at[k, h], (w, right))

    def ring_left(k, h):
        o = along(h)
        return remote(gathered.at[k, o], gathered.at[k, o], left_send.at[k, h], left_recv.at[k, h], (w, left))

    def ring_right_in(k, h):
        o = along(-h - 1)
        return remote(gathered.at[k, o], gathered.at[k, o], right_send.at[k, h], right_recv.at[k, h], (w, right))

    def ring_left_in(k, h):
        o = along(h + 1)
        return remote(gathered.at[k, o], gathered.at[k, o], left_send.at[k, h], left_recv.at[k, h], (w, left))

    def ask_right(h):
        o = along(-h)
        return remote(asked.at[o], asked.at[o], ask_rsend.at[h], ask_rrecv.at[h], (w, right))

    def ask_left(h):
        o = along(h)
        return remote(asked.at[o], asked.at[o], ask_lsend.at[h], ask_lrecv.at[h], (w, left))

    def ask_right_in(h):
        o = along(-h - 1)
        return remote(asked.at[o], asked.at[o], ask_rsend.at[h], ask_rrecv.at[h], (w, right))

    def ask_left_in(h):
        o = along(h + 1)
        return remote(asked.at[o], asked.at[o], ask_lsend.at[h], ask_lrecv.at[h], (w, left))

    base_copy = remote(base.at[c], base.at[c], base_send, base_recv, (w, other))
    base_in = remote(base.at[1 - c], base.at[1 - c], base_send, base_recv, (w, other))
    far_copy = remote(sol, sol_far, far_send, far_recv, (far, q))
    diag_copy = pltpu.make_async_copy(inverse, diag, diag_sem)
    ask_copy = pltpu.make_async_copy(demand.at[w], asked.at[z], ask_own)

    def part_copy(k, i, col, core):
        return remote(contrib.at[k], partial.at[col, c], part_send.at[k, core], part_recv.at[col, c], (i, 2 * z + core))

    def part_in(col, core):
        return remote(contrib.at[0], partial.at[col, core], part_send.at[0, 0], part_recv.at[col, core], (w, other))

    ask_copy.start()
    for k in range(n2):
        @pl.when(jnp.logical_and(k < count, jnp.logical_not(is_moved(k))))
        def _():
            local_tile(k).start()
    diag_copy.start()

    barrier = pltpu.get_barrier_semaphore()
    me = 2 * w + c

    def greet_plane(d, carry):
        t = lax.rem(me + d, 2 * n)
        pl.semaphore_signal(barrier, inc=1, device_id=(t // 2, 2 * z + t % 2), device_id_type=MESH)
        return carry

    lax.fori_loop(1, 2 * n, greet_plane, 0)
    for side in (right, left):
        pl.semaphore_signal(barrier, inc=1, device_id=(w, side), device_id_type=MESH)
    diag_copy.wait()
    span, lane = 8 * rows, 4 * rows
    m = lax.broadcasted_iota(jnp.int32, (2 * rows, rows), 0)
    t = lax.broadcasted_iota(jnp.int32, (2 * rows, rows), 1)
    pick[...] = jnp.zeros_like(pick)
    for core in range(2):
        unit = (m == t + core * rows).astype(jnp.bfloat16)
        for b in range(4):
            lo = core * lane + b * rows
            pick[2 * rows * b:2 * rows * (b + 1), lo:lo + rows] = unit
    for u in range(diag.shape[1] // span):
        moved = jnp.dot(
            diag[:, u * span:(u + 1) * span], pick[...], preferred_element_type=jnp.float32
        ).astype(jnp.bfloat16)
        diag_split[0, :, u * lane:(u + 1) * lane] = moved[:, :lane]
        diag_split[1, :, u * lane:(u + 1) * lane] = moved[:, lane:]
    pl.semaphore_wait(barrier, 2 * n - 1 + 2)

    def gives(k):
        return jnp.logical_and(low, k < n2 - 1 - j)

    for k in range(n2 - 1):
        @pl.when(gives(k))
        def _():
            moved_tile(k, w + jnp.where(k == n2 - 2 - j, span_j - 1, 2 * k + 3)).start()
    ask_copy.wait()

    def solve(i):
        base_in.wait_recv()

        def add(col, acc):
            a, b = acc
            part_in(col, 0).wait_recv()
            part_in(col, 1).wait_recv()
            return a + partial[col, 0].astype(jnp.float32), b + partial[col, 1].astype(jnp.float32)

        zero = jnp.zeros((cols, half), jnp.float32)
        a, b = lax.fori_loop(0, i, add, (zero, zero))
        a = (base[0].astype(jnp.float32) - a).astype(jnp.bfloat16)
        b = (base[1].astype(jnp.float32) - b).astype(jnp.bfloat16)
        y = (dot_nt(a, diag_split[0]) + dot_nt(b, diag_split[1])).astype(jnp.bfloat16)
        sol[...] = y
        sol_split[0] = y[:, :half]
        sol_split[1] = y[:, half:]

        @pl.when(w < n2 - 1)
        def _():
            far_copy.start()

    def apply(k, use_far):
        col = jnp.where(use_far, far, w)
        y = jnp.where(use_far, sol_far[...], sol[...])
        ring_right_in(k, hops - 1).wait_recv()
        tile = gathered[k].reshape(half, gathered.shape[3])
        contrib[k] = dot_nt(y, tile).astype(jnp.bfloat16)
        row = row_of(k)
        part_copy(k, row, col, 0).start()
        part_copy(k, row, col, 1).start()

    def row_step(i):
        last = i // 2
        own_event = i == w
        far_event = jnp.logical_and(jnp.logical_not(low), jnp.logical_and(i == j + 2, shared > 0))
        since = jnp.where(is_moved(last), j + 2, w)
        ready = jnp.logical_and(lax.rem(i, 2) == 0, jnp.logical_and(last < count, i > since))
        start = jnp.where(own_event, jnp.where(low, 0, shared), jnp.where(far_event, 0, last))
        stop = jnp.where(
            own_event,
            jnp.minimum(last, count - 1),
            jnp.where(far_event, jnp.minimum(last, shared - 1), jnp.where(ready, last, start - 1)),
        )

        @pl.when(own_event)
        def _():
            solve(i)

        @pl.when(far_event)
        def _():
            far_copy.wait_recv()

        use_far = is_moved(start)

        def step(k, carry):
            apply(k, use_far)
            return carry

        lax.fori_loop(start, stop + 1, step, 0)

    def ring_slot(u, parity):
        for m in range(hops // 2, -1, -1):
            h = parity + 2 * m
            if h >= hops:
                continue
            k = u - m

            @pl.when(jnp.logical_and(k >= 0, k < count))
            def _():
                if h == 0:
                    @pl.when(is_moved(k))
                    def _():
                        moved_tile(k, 0).wait_recv()

                    @pl.when(jnp.logical_not(is_moved(k)))
                    def _():
                        local_tile(k).wait()
                else:
                    ring_right_in(k, h - 1).wait_recv()
                ring_right(k, h).start()
                if h > 0:
                    ring_left_in(k, h - 1).wait_recv()
                if h < hops - 1:
                    ring_left(k, h).start()

    def ask_slot(t):
        @pl.when(t == 0)
        def _():
            ask_right(0).start()
            ask_left(0).start()

        @pl.when(jnp.logical_and(t > 0, t < hops))
        def _():
            ask_right_in(t - 1).wait_recv()
            ask_right(t).start()
            ask_left_in(t - 1).wait_recv()

            @pl.when(t < hops - 1)
            def _():
                ask_left(t).start()

        @pl.when(t == hops - 1)
        def _():
            ask_right_in(t).wait_recv()
            wide = asked.shape[2]
            mine = (
                lax.broadcasted_iota(jnp.int32, (cols, wide), 1)
                == cols * z + lax.broadcasted_iota(jnp.int32, (cols, wide), 0)
            ).astype(jnp.bfloat16)
            base[c] = dot_nt(mine, asked[...].reshape(half, wide)).astype(jnp.bfloat16)
            base_copy.start()

    def slot_pair(u, carry):
        for parity in range(2):
            t = 2 * u + parity

            @pl.when(t < hops)
            def _():
                ask_slot(t)

            ring_slot(u, parity)
            i = t - (hops - 1)

            @pl.when(jnp.logical_and(i >= 0, i < n))
            def _():
                row_step(i)

        return carry

    lax.fori_loop(0, (n + hops) // 2, slot_pair, 0)

    def out_copy(d):
        t = lax.rem(z + d, nz)
        spot = result.at[c, z // 4, z % 4]
        return remote(sol_split.at[c], spot, out_send.at[d], out_recv.at[d], (w, 2 * t + c))

    def out_in(d):
        t = lax.rem(z - d + nz, nz)
        spot = result.at[c, t // 4, t % 4]
        return remote(sol_split.at[c], spot, out_send.at[d], out_recv.at[d], (w, 2 * t + c))

    def group_copy(d):
        mine = result.at[c, :, z % 4]
        t = lax.rem(z + d, nz)
        return remote(mine, mine, out_send.at[d], out_recv.at[d], (w, 2 * t + c))

    def group_in(d):
        t = lax.rem(z - d + nz, nz)
        theirs = result.at[c, :, t % 4]
        return remote(theirs, theirs, out_send.at[d], out_recv.at[d], (w, 2 * z + 1 - c))

    strides = sorted(range(4, nz, 4), key=lambda d: -min(d, nz - d))
    nears = (2, 1, nz - 1)
    for d in strides:
        out_copy(d).start()
    result[c, z // 4, z % 4] = sol_split[c]
    for d in strides:
        out_in(d).wait_recv()
    for d in nears:
        group_copy(d).start()
    for d in nears:
        group_in(d).wait_recv()
    swap = remote(result.at[c], result.at[c], swap_send, swap_recv, (w, other))
    swap.start()

    for k in range(n2 - 1):
        @pl.when(gives(k))
        def _():
            moved_tile(k, w + jnp.where(k == n2 - 2 - j, span_j - 1, 2 * k + 3)).wait_send()
    for k in range(n2):
        @pl.when(k < count)
        def _():
            for h in range(hops):
                ring_right(k, h).wait_send()
            for h in range(hops - 1):
                ring_left(k, h).wait_send()
            part_copy(k, 0, 0, 0).wait_send()
            part_copy(k, 0, 0, 1).wait_send()
    for h in range(hops):
        ask_right(h).wait_send()
    for h in range(hops - 1):
        ask_left(h).wait_send()
    base_copy.wait_send()

    @pl.when(w < n2 - 1)
    def _():
        far_copy.wait_send()

    for d in strides:
        out_copy(d).wait_send()
    for d in nears:
        group_copy(d).wait_send()
    swap.wait_send()
    remote(result.at[1 - c], result.at[1 - c], swap_send, swap_recv, (w, other)).wait_recv()
    for s in range(2):
        out[:, s * half:(s + 1) * half] = result[s].reshape(nz * cols, half)


def on_device(factor_tiles, inverse_blocks, demand):
    n, rows, _, _, width = factor_tiles.shape
    nz = lax.axis_size("pcol") // 2
    wide = demand.shape[2]
    cols = wide // nz
    half = width // 2
    n2, hops = n // 2, nz // 2
    dma = pltpu.SemaphoreType.DMA
    out = pl.pallas_call(
        functools.partial(kernel, n, nz, cols, rows),
        out_shape=jax.ShapeDtypeStruct((wide, width), jnp.bfloat16),
        in_specs=[pl.BlockSpec(memory_space=pltpu.HBM)] * 3,
        out_specs=pl.BlockSpec(memory_space=pltpu.VMEM),
        scratch_shapes=[
            pltpu.VMEM((n2, nz, rows, width), jnp.bfloat16),
            pltpu.VMEM((width, width), jnp.bfloat16),
            pltpu.VMEM((2, width, half), jnp.bfloat16),
            pltpu.VMEM((nz, rows, wide), jnp.bfloat16),
            pltpu.VMEM((2, cols, half), jnp.bfloat16),
            pltpu.VMEM((n, 2, cols, half), jnp.bfloat16),
            pltpu.VMEM((cols, width), jnp.bfloat16),
            pltpu.VMEM((2, cols, half), jnp.bfloat16),
            pltpu.VMEM((cols, width), jnp.bfloat16),
            pltpu.VMEM((n2, cols, half), jnp.bfloat16),
            pltpu.VMEM((2, nz // 4, 4, cols, half), jnp.bfloat16),
            pltpu.VMEM((8 * rows, 8 * rows), jnp.bfloat16),
            dma((n2,)), dma((n2,)),
            dma((n2, hops)), dma((n2, hops)), dma((n2, hops - 1)), dma((n2, hops - 1)),
            dma, dma((hops,)), dma((hops,)), dma((hops - 1,)), dma((hops - 1,)),
            dma, dma, dma, dma((n2, 2)), dma((n, 2)),
            dma, dma, dma((nz,)), dma((nz,)), dma, dma,
        ],
        compiler_params=pltpu.CompilerParams(
            collective_id=0, has_side_effects=True
        ),
    )(
        factor_tiles.reshape(n, rows, width),
        inverse_blocks.reshape(width, width),
        demand,
    )
    return out.T.reshape(1, 1, width, wide)


def solution(mesh):
    placed = (
        P(None, "pcol", None, "prow", None),
        P(None, "prow", None, None),
        P(None, "pcol", None),
    )
    return jax.shard_map(
        on_device,
        mesh=mesh,
        in_specs=placed,
        out_specs=P(None, "prow", None, None),
        check_vma=False,
    )
```
